32 devices in a mesh: dp: 4 (over y, x), ctx: 8 (over z, core).
Axes of the slice: x: 2, y: 2, z: 4, core: 2. Of those that a mesh axis runs over, the one named last changes fastest.
Arguments:
- hidden: bfloat16 [4, 4096, 8192], P('dp', 'ctx'), may hold values from -8 to 8
- norm_gain: float32 [8192], replicated, may hold values from 0.3 to 5.2
- cotangent: bfloat16 [4, 4096, 512], P('dp', 'ctx'), may hold values from -30 to 30
- loss_weight: float32 [4], P('dp'), may hold values from 0.08 to 5
Outputs:
- clipped_grad: float32 [8192, 512], P('ctx', 'dp')
The draws below stay inside these ranges and needn't reach their ends.
All inputs are finite; a program needn't handle non-finite values.
Results may differ from the reference program's by a relative error of at most 0.0022.
Values may be sent and summed in bfloat16 or wider, within the bound.
A program may use at most 64 MiB of HBM per device.

```python
import math
from functools import partial
import jax
import jax.numpy as jnp
from jax import lax

D = 8192
OUT = 512
LENGTH = 4096
EXAMPLES = 4


def draw_hidden(key, part):
    base_key = jax.random.fold_in(key, 41)
    mean_key = jax.random.fold_in(key, 42)
    shared = jax.random.truncated_normal(mean_key, -4.0, 4.0, (EXAMPLES, 1, D), jnp.float32)
    base = jax.random.truncated_normal(base_key, -6.0, 6.0, (EXAMPLES, LENGTH, D), jnp.float32)
    return (base + 0.5 * shared).astype(jnp.bfloat16)


def draw_norm_gain(key, part):
    first_key = jax.random.fold_in(key, 11)
    ramp = jnp.sqrt(1.0 + 2.0 * jnp.arange(D, dtype=jnp.float32) / D)
    rough = jnp.exp(jax.random.uniform(first_key, (D,), jnp.float32, math.log(0.3), math.log(3.0)))
    return (ramp * rough).astype(jnp.float32)


def draw_cotangent(key, part):
    scale_key = jax.random.fold_in(key, 21)
    base_key = jax.random.fold_in(key, 22)
    common_key = jax.random.fold_in(key, 23)
    column_scale = jnp.exp(jax.random.uniform(scale_key, (OUT,), jnp.float32, math.log(0.3), math.log(3.0)))
    shared = jax.random.truncated_normal(common_key, -6.0, 6.0, (EXAMPLES, 1, OUT), jnp.float32)
    base = jax.random.truncated_normal(base_key, -6.0, 6.0, (EXAMPLES, LENGTH, OUT), jnp.float32)
    base = base + 2.0 / math.sqrt(LENGTH) * shared
    return (base * column_scale).astype(jnp.bfloat16)


def draw_loss_weight(key, part):
    order_key = jax.random.fold_in(key, 31)
    small_key = jax.random.fold_in(key, 32)
    large_key = jax.random.fold_in(key, 33)
    order = jax.random.permutation(order_key, EXAMPLES)
    small = jnp.exp(jax.random.uniform(small_key, (EXAMPLES,), jnp.float32, math.log(0.08), math.log(0.2)))
    large = jnp.exp(jax.random.uniform(large_key, (EXAMPLES,), jnp.float32, math.log(1.5), math.log(5.0)))
    return jnp.where(order % 2 == 0, small, large).astype(jnp.float32)


def setup_inputs(seed: int = 0) -> dict:
    arg_keys = jax.random.split(jax.random.key(seed), 5)
    hidden = draw_hidden(jax.random.fold_in(arg_keys[4], 71), 0)
    norm_gain = draw_norm_gain(jax.random.fold_in(arg_keys[4], 71), 0)
    cotangent = draw_cotangent(jax.random.fold_in(arg_keys[4], 71), 0)
    loss_weight = draw_loss_weight(jax.random.fold_in(arg_keys[4], 71), 0)
    return dict(hidden=hidden, norm_gain=norm_gain, cotangent=cotangent, loss_weight=loss_weight)


def per_example(gain_vector, bundle):
    values, upstream, weight = bundle
    widened = values.astype(jnp.float32)
    scale = lax.rsqrt(lax.optimization_barrier(jnp.mean(widened * widened, axis=1, keepdims=True)) + 1e-05)
    normed = (widened * scale * gain_vector).astype(jnp.bfloat16)
    product = lax.dot_general(normed, upstream, (((0,), (0,)), ((), ())), preferred_element_type=jnp.float32)
    return product * (weight / math.sqrt(LENGTH))

def reference(hidden, norm_gain, cotangent, loss_weight):
    grads = lax.map(partial(per_example, norm_gain), (hidden, cotangent, loss_weight))
    squares = lax.optimization_barrier(jnp.sum(grads * grads, axis=(1, 2)))
    clip_bound = math.sqrt(D * OUT)
    factor = jnp.minimum(1.0, clip_bound * lax.rsqrt(squares + 1e-06))
    return lax.optimization_barrier(jnp.sum(factor[:, None, None] * grads, axis=0))
```

```python
import functools
import math

import jax
import jax.numpy as jnp
from jax import lax
from jax.experimental import pallas as pl
from jax.experimental.pallas import tpu as pltpu
from jax.sharding import PartitionSpec as P

MESH = pl.DeviceIdType.MESH
CORES = 2
LAG = 2


def per_device(hidden, norm_gain, cotangent, loss_weight):
    widened = hidden[0].astype(jnp.float32)
    scale = lax.rsqrt(jnp.mean(widened * widened, axis=1, keepdims=True) + 1e-05)
    normed = (widened * scale * norm_gain).astype(jnp.bfloat16)
    upstream = cotangent[0]
    context_size = lax.axis_size("ctx")
    doc_length = upstream.shape[0] * context_size
    weight = loss_weight[0] / math.sqrt(doc_length)
    features = normed.shape[1]
    outputs = upstream.shape[1]
    contract = (((0,), (0,)), ((), ()))
    owned_tile = lax.psum_scatter(
        weight * lax.dot_general(normed, upstream, contract, preferred_element_type=jnp.float32),
        "ctx",
        scatter_dimension=0,
        tiled=True,
    )
    squares = jnp.sum(owned_tile * owned_tile)
    clip_bound = math.sqrt(features * outputs)
    summed = lax.psum(squares, "ctx")
    factor = jnp.minimum(1.0, clip_bound * lax.rsqrt(summed + 1e-06))
    result = lax.psum_scatter(factor * owned_tile, "dp", scatter_dimension=1, tiled=True)
    return result


def kernel(
    cfg,
    hid_ref,
    gain_ref,
    cot_ref,
    w_ref,
    out_ref,
    nm,
    pn,
    ct,
    acc,
    sbuf,
    rbuf,
    fin,
    dpbuf,
    sqacc,
    sqbuf,
    relsend,
    relrecv,
    xs,
    xr,
    cs,
    cr,
    zs,
    zr,
    ds_,
    dr,
    ss,
    sr,
    rs,
    rr,
):
    (tokens, features, outs, line, ndp, oc, fc, rows, inv_len, bound) = cfg
    block = features // (CORES * line)
    half = features // CORES // 2
    ftiles = half // fc
    ohalves = outs // oc
    chunks = ftiles * ohalves
    owned = outs // ndp
    per_half = oc // owned
    dp = lax.axis_index("dp")
    ctx = lax.axis_index("ctx")
    q = ctx // CORES
    k = ctx % CORES
    other = ctx - k + (1 - k)
    side = q // (line - 1)
    is_end = (q == 0) | (q == line - 1)
    down = ctx - CORES
    up = ctx + CORES

    ends = []
    for a in range(ndp):
        for b in range(2):
            for c in range(CORES):
                if a + b + c > 0:
                    pos = ((side + b) % 2) * (line - 1) * CORES + (k + c) % CORES
                    ends.append(((a * 2 + b) * CORES + c, ((dp + a) % ndp, pos)))

    bar = pltpu.get_barrier_semaphore()
    pl.semaphore_signal(bar, inc=1, device_id=(dp, other), device_id_type=MESH)

    @pl.when(q > 0)
    def _():
        pl.semaphore_signal(bar, inc=1, device_id=(dp, down), device_id_type=MESH)

    @pl.when(q < line - 1)
    def _():
        pl.semaphore_signal(bar, inc=1, device_id=(dp, up), device_id_type=MESH)

    @pl.when(is_end)
    def _():
        for slot, peer in ends:
            if slot != 1:
                pl.semaphore_signal(bar, inc=1, device_id=peer, device_id_type=MESH)
        pl.semaphore_wait(bar, len(ends) + 1)

    @pl.when(jnp.logical_not(is_end))
    def _():
        pl.semaphore_wait(bar, 3)

    ct[0] = cot_ref[...].T
    cot_copy = pltpu.make_async_remote_copy(
        src_ref=ct.at[0], dst_ref=ct.at[1], send_sem=cs, recv_sem=cr,
        device_id=(dp, other), device_id_type=MESH,
    )
    cot_copy.start()

    groups = xs.shape[0]
    grows = tokens // groups

    def norm_copy(g):
        at = pl.ds(pl.multiple_of(g * grows, grows), grows)
        return pltpu.make_async_remote_copy(
            src_ref=nm.at[1 - k, at], dst_ref=pn.at[at], send_sem=xs.at[g], recv_sem=xr.at[g],
            device_id=(dp, other), device_id_type=MESH,
        )

    def norm_rows(i, carry):
        at = pl.ds(pl.multiple_of(i * rows, rows), rows)
        total = jnp.zeros((rows, block), jnp.float32)
        for j in range(CORES * line):
            v = hid_ref[at, j * block : (j + 1) * block].astype(jnp.float32)
            total = total + v * v
        mean = jnp.sum(total, axis=1, keepdims=True) * (1.0 / features)
        scale = lax.rsqrt(mean + 1e-05)
        for j in range(CORES * line):
            v = hid_ref[at, j * block : (j + 1) * block].astype(jnp.float32)
            g = gain_ref[:, j * block : (j + 1) * block]
            local = (j // CORES) * block
            nm[j % CORES, at, local : local + block] = (v * scale * g).astype(jnp.bfloat16)
        return carry

    def norm_group(g, carry):
        per = grows // rows
        lax.fori_loop(g * per, (g + 1) * per, norm_rows, 0)
        norm_copy(g).start()
        return carry

    lax.fori_loop(0, groups, norm_group, 0)
    sqacc[...] = jnp.zeros_like(sqacc)
    cot_copy.wait()
    lax.fori_loop(0, groups, lambda g, c: (norm_copy(g).wait(), c)[1], 0)

    def z_copy(d, s):
        return pltpu.make_async_remote_copy(
            src_ref=sbuf.at[d, s], dst_ref=rbuf.at[d, s], send_sem=zs.at[d, s],
            recv_sem=zr.at[d, s], device_id=(dp, down if d == 0 else up), device_id_type=MESH,
        )

    def dp_copy(a, ft):
        d = (dp + a) % ndp
        return pltpu.make_async_remote_copy(
            src_ref=fin.at[pl.ds(pl.multiple_of(d * owned, owned), owned),
                           pl.ds(pl.multiple_of(ft * fc, fc), fc)],
            dst_ref=dpbuf.at[a - 1, :, pl.ds(pl.multiple_of(ft * fc, fc), fc)],
            send_sem=ds_.at[a - 1, ft], recv_sem=dr.at[a - 1, ft],
            device_id=(d, ctx), device_id_type=MESH,
        )

    def process(d, s):
        ft = s // ohalves
        h = s % ohalves
        local = pl.ds(pl.multiple_of(d * half + ft * fc, fc), fc)
        orow = pl.ds(pl.multiple_of(h * oc, oc), oc)
        first = q == (line - 1 if d == 0 else 0)
        last = q == (0 if d == 0 else line - 1)
        acc[d] = jnp.dot(
            ct[0, orow, :], nm[k, :, local], preferred_element_type=jnp.float32
        ) + jnp.dot(ct[1, orow, :], pn[:, local], preferred_element_type=jnp.float32)

        @pl.when(first)
        def _():
            sbuf[d, s] = acc[d].astype(jnp.bfloat16)
            z_copy(d, s).start()

        @pl.when(jnp.logical_not(first | last))
        def _():
            z_copy(d, s).wait_recv()
            sbuf[d, s] = (acc[d] + rbuf[d, s].astype(jnp.float32)).astype(jnp.bfloat16)
            z_copy(d, s).start()

        @pl.when(last)
        def _():
            z_copy(d, s).wait_recv()
            tile = acc[d] + rbuf[d, s].astype(jnp.float32)
            fin[orow, pl.ds(pl.multiple_of(ft * fc, fc), fc)] = tile
            sqacc[...] += jnp.sum((tile * tile).reshape(oc // 8, 8, fc), axis=0)
            for a in range(1, ndp):

                @pl.when(((dp + a) % ndp) // per_half == h)
                def _():
                    dp_copy(a, ft).start()

    def step(t, carry):
        for d in range(2):
            s = t - ((line - 1 - q) if d == 0 else q) * LAG

            @pl.when((s >= 0) & (s < chunks))
            def _():
                process(d, s)

        return carry

    lax.fori_loop(0, chunks + (line - 1) * LAG, step, 0)

    def z_done(s, carry):
        @pl.when(q > 0)
        def _():
            z_copy(0, s).wait_send()

        @pl.when(q < line - 1)
        def _():
            z_copy(1, s).wait_send()

        return carry

    def rel_copy(i, to):
        at = pl.ds(i * fc, fc)
        return pltpu.make_async_remote_copy(
            src_ref=relsend.at[at], dst_ref=relrecv.at[at], send_sem=rs.at[i], recv_sem=rr.at[i],
            device_id=(dp, to), device_id_type=MESH,
        )

    rtiles = block // fc

    def ending(sd):
        toward = up if sd == 0 else down
        weight = w_ref[0, 0] * inv_len
        sq = jnp.sum(jnp.sum(sqacc[...], axis=1, keepdims=True), axis=0, keepdims=True)
        row = lax.broadcasted_iota(jnp.int32, (8, 128), 0)
        sqbuf[0] = jnp.where(row == 0, jnp.broadcast_to(sq * (weight * weight), (8, 128)), weight)
        sends = [
            pltpu.make_async_remote_copy(
                src_ref=sqbuf.at[0], dst_ref=sqbuf.at[slot], send_sem=ss.at[slot - 1],
                recv_sem=sr.at[slot - 1], device_id=peer, device_id_type=MESH,
            )
            for slot, peer in ends
        ]
        for c in sends:
            c.start()
        for a in range(1, ndp):
            lax.fori_loop(0, ftiles, lambda ft, c, a=a: (dp_copy(a, ft).wait(), c)[1], 0)
        for c in sends:
            c.wait()
        mult = []
        for a in range(ndp):
            base = a * 2 * CORES
            total = sqbuf[base, 0:1, :]
            for i in range(1, 2 * CORES):
                total = total + sqbuf[base + i, 0:1, :]
            factor = jnp.minimum(1.0, bound * lax.rsqrt(total + 1e-06))
            mult.append((factor * sqbuf[base, 1:2, :])[:, 0:1])
        mine = pl.ds(pl.multiple_of(dp * owned, owned), owned)

        def combine(f0):
            cols = slice(f0, f0 + fc)
            value = fin[mine, cols] * mult[0]
            for a in range(1, ndp):
                value = value + dpbuf[a - 1, :, cols] * mult[a]
            return value.T

        far, near = (block, 0) if sd == 0 else (0, block)
        for i in range(rtiles):
            relsend[i * fc : (i + 1) * fc, :] = combine(far + i * fc)
            rel_copy(i, toward).start()
        for i in range(rtiles):
            out_ref[i * fc : (i + 1) * fc, :] = combine(near + i * fc)
        lax.fori_loop(0, chunks, z_done, 0)
        for i in range(rtiles):
            rel_copy(i, toward).wait_send()

    @pl.when(q == 0)
    def _():
        ending(0)

    @pl.when(q == line - 1)
    def _():
        ending(1)

    @pl.when(jnp.logical_not(is_end))
    def _():
        lax.fori_loop(0, chunks, z_done, 0)
        for i in range(rtiles):
            rel_copy(i, down).wait_recv()
            out_ref[i * fc : (i + 1) * fc, :] = relrecv[i * fc : (i + 1) * fc, :]


def fused(hidden, norm_gain, cotangent, loss_weight):
    _, tokens, features = hidden.shape
    outs = cotangent.shape[2]
    ctx = lax.axis_size("ctx")
    ndp = lax.axis_size("dp")
    line = ctx // CORES
    block = features // ctx
    half = features // CORES // 2
    owned = outs // ndp
    oc, fc, rows, groups = outs // 2, 256, 16, 4
    ftiles = half // fc
    chunks = ftiles * (outs // oc)
    cfg = (tokens, features, outs, line, ndp, oc, fc, rows,
           1.0 / math.sqrt(tokens * ctx), math.sqrt(features * outs))
    bf16, f32 = jnp.bfloat16, jnp.float32
    dma = pltpu.SemaphoreType.DMA
    vmem = pl.BlockSpec(memory_space=pltpu.VMEM)
    return pl.pallas_call(
        functools.partial(kernel, cfg),
        name="clipped_grad",
        out_shape=jax.ShapeDtypeStruct((block, owned), f32),
        in_specs=[vmem, vmem, vmem, pl.BlockSpec(memory_space=pltpu.SMEM)],
        out_specs=vmem,
        scratch_shapes=[
            pltpu.VMEM((CORES, tokens, features // CORES), bf16),
            pltpu.VMEM((tokens, features // CORES), bf16),
            pltpu.VMEM((CORES, outs, tokens), bf16),
            pltpu.VMEM((2, oc, fc), f32),
            pltpu.VMEM((2, chunks, oc, fc), bf16),
            pltpu.VMEM((2, chunks, oc, fc), bf16),
            pltpu.VMEM((outs, half), f32),
            pltpu.VMEM((ndp - 1, owned, half), f32),
            pltpu.VMEM((8, fc), f32),
            pltpu.VMEM((ndp * 2 * CORES, 8, 128), f32),
            pltpu.VMEM((block, owned), f32),
            pltpu.VMEM((block, owned), f32),
            dma((groups,)), dma((groups,)),
            dma(()), dma(()),
            dma((2, chunks)), dma((2, chunks)),
            dma((ndp - 1, ftiles)), dma((ndp - 1, ftiles)),
            dma((ndp * 2 * CORES - 1,)), dma((ndp * 2 * CORES - 1,)),
            dma((block // fc,)), dma((block // fc,)),
        ],
        compiler_params=pltpu.CompilerParams(
            collective_id=0, has_side_effects=True, vmem_limit_bytes=60 << 20
        ),
    )(hidden[0], norm_gain[None, :], cotangent[0], loss_weight[None, :])


def solution(mesh):
    in_specs = (P("dp", "ctx", None), P(), P("dp", "ctx", None), P("dp"))
    out_specs = P("ctx", "dp")
    body = fused if mesh.shape["ctx"] == 4 * CORES else per_device
    return jax.shard_map(body, mesh=mesh, in_specs=in_specs, out_specs=out_specs, check_vma=False)
```

```python
import functools
import math

import jax
import jax.numpy as jnp
from jax import lax
from jax.experimental import pallas as pl
from jax.experimental.pallas import tpu as pltpu
from jax.sharding import PartitionSpec as P

MESH = pl.DeviceIdType.MESH
CORES = 2
LAG = 4


def per_device(hidden, norm_gain, cotangent, loss_weight):
    widened = hidden[0].astype(jnp.float32)
    scale = lax.rsqrt(jnp.mean(widened * widened, axis=1, keepdims=True) + 1e-05)
    normed = (widened * scale * norm_gain).astype(jnp.bfloat16)
    upstream = cotangent[0]
    context_size = lax.axis_size("ctx")
    doc_length = upstream.shape[0] * context_size
    weight = loss_weight[0] / math.sqrt(doc_length)
    features = normed.shape[1]
    outputs = upstream.shape[1]
    contract = (((0,), (0,)), ((), ()))
    owned_tile = lax.psum_scatter(
        weight * lax.dot_general(normed, upstream, contract, preferred_element_type=jnp.float32),
        "ctx",
        scatter_dimension=0,
        tiled=True,
    )
    squares = jnp.sum(owned_tile * owned_tile)
    clip_bound = math.sqrt(features * outputs)
    summed = lax.psum(squares, "ctx")
    factor = jnp.minimum(1.0, clip_bound * lax.rsqrt(summed + 1e-06))
    result = lax.psum_scatter(factor * owned_tile, "dp", scatter_dimension=1, tiled=True)
    return result


def flip(v, m):
    return ((v // 2 + m // 2) % 2) * 2 + (v % 2 + m % 2) % 2


def kernel(
    cfg,
    hid_ref,
    gain_ref,
    cot_ref,
    w_ref,
    out_ref,
    hv,
    pr,
    ct,
    sc,
    nt,
    acc,
    sbuf,
    rbuf,
    fin,
    dpbuf,
    sqacc,
    sqbuf,
    relsend,
    relrecv,
    ls,
    xs,
    xr,
    es,
    er,
    zs,
    zr,
    ds_,
    dr,
    ss,
    sr,
    rs,
    rr,
):
    (tokens, features, outs, line, ndp, fc, rows, inv_len, bound) = cfg
    block = features // (CORES * line)
    half = features // CORES // 2
    ftiles = half // fc
    owned = outs // ndp
    chunks = ftiles * ndp
    groups = ls.shape[0]
    grows = tokens // groups
    pieces = xs.shape[0] // 2
    pw = half // pieces
    dp = lax.axis_index("dp")
    ctx = lax.axis_index("ctx")
    q = ctx // CORES
    k = ctx % CORES
    other = ctx - k + (1 - k)
    side = q // (line - 1)
    is_end = (q == 0) | (q == line - 1)
    down = ctx - CORES
    up = ctx + CORES

    ends = []
    for a in range(ndp):
        for b in range(2):
            for c in range(CORES):
                if a + b + c > 0:
                    pos = ((side + b) % 2) * (line - 1) * CORES + (k + c) % CORES
                    ends.append(((a * 2 + b) * CORES + c, (flip(dp, a), pos)))

    bar = pltpu.get_barrier_semaphore()
    pl.semaphore_signal(bar, inc=1, device_id=(dp, other), device_id_type=MESH)

    @pl.when(q > 0)
    def _():
        pl.semaphore_signal(bar, inc=1, device_id=(dp, down), device_id_type=MESH)

    @pl.when(q < line - 1)
    def _():
        pl.semaphore_signal(bar, inc=1, device_id=(dp, up), device_id_type=MESH)

    @pl.when(is_end)
    def _():
        for slot, peer in ends:
            if slot != 1:
                pl.semaphore_signal(bar, inc=1, device_id=peer, device_id_type=MESH)

    def load(g):
        at = pl.ds(pl.multiple_of(g * grows, grows), grows)
        return pltpu.make_async_copy(hid_ref.at[at], hv.at[at], ls.at[g])

    for g in range(groups):
        load(g).start()
    ct[0] = cot_ref[...].T

    @pl.when(is_end)
    def _():
        pl.semaphore_wait(bar, len(ends) + 1)

    @pl.when(jnp.logical_not(is_end))
    def _():
        pl.semaphore_wait(bar, 3)

    def place(d, local, core):
        return (CORES * (d * (line // 2) + local // block) + core) * block + local % block

    def piece_copy(d, p):
        src = pl.ds(pl.multiple_of(place(d, p * pw, 1 - k), pw), pw)
        return pltpu.make_async_remote_copy(
            src_ref=hid_ref.at[:, src], dst_ref=pr.at[:, pl.ds(d * half + p * pw, pw)],
            send_sem=xs.at[2 * p + d], recv_sem=xr.at[2 * p + d],
            device_id=(dp, other), device_id_type=MESH,
        )

    def extra_copy(buf, i):
        return pltpu.make_async_remote_copy(
            src_ref=buf.at[0], dst_ref=buf.at[1], send_sem=es.at[i], recv_sem=er.at[i],
            device_id=(dp, other), device_id_type=MESH,
        )

    for p in range(pieces):
        for d in range(2):
            piece_copy(d, p).start()
        if p == 0:
            extra_copy(ct, 0).start()

    def stat_rows(i, carry):
        at = pl.ds(pl.multiple_of(i * rows, rows), rows)
        total = jnp.zeros((rows, block), jnp.float32)
        for j in range(CORES * line):
            v = hv[at, j * block : (j + 1) * block].astype(jnp.float32)
            total = total + v * v
        mean = jnp.sum(total, axis=1, keepdims=True) * (1.0 / features)
        sc[0, at, :] = jnp.broadcast_to(lax.rsqrt(mean + 1e-05), (rows, 128))
        return carry

    def stat_group(g, carry):
        load(g).wait()
        per = grows // rows
        lax.fori_loop(g * per, (g + 1) * per, stat_rows, 0)
        return carry

    lax.fori_loop(0, groups, stat_group, 0)
    extra_copy(sc, 1).start()
    sqacc[...] = jnp.zeros_like(sqacc)
    extra_copy(ct, 0).wait()
    extra_copy(sc, 1).wait()

    def z_copy(d, s):
        return pltpu.make_async_remote_copy(
            src_ref=sbuf.at[d, s], dst_ref=rbuf.at[d, s], send_sem=zs.at[d, s],
            recv_sem=zr.at[d, s], device_id=(dp, down if d == 0 else up), device_id_type=MESH,
        )

    def dp_copy(m, ft):
        h = flip(dp, m)
        cols = pl.ds(pl.multiple_of(ft * fc, fc), fc)
        return pltpu.make_async_remote_copy(
            src_ref=fin.at[pl.ds(pl.multiple_of(h * owned, owned), owned), cols],
            dst_ref=dpbuf.at[m - 1, :, cols],
            send_sem=ds_.at[m - 1, ft], recv_sem=dr.at[m - 1, ft],
            device_id=(h, ctx), device_id_type=MESH,
        )

    def multiply(d, ft):
        for p in range(pieces):

            @pl.when(ft * fc == p * pw)
            def _():
                piece_copy(d, p).wait()

        own = pl.multiple_of(place(d, ft * fc, k), fc)
        got = pl.multiple_of(d * half + ft * fc, fc)

        def norm_rows(i, carry):
            at = pl.ds(pl.multiple_of(i * 64, 64), 64)
            low = pl.ds(pl.multiple_of(tokens + i * 64, 64), 64)
            for c in range(0, fc, 128):
                g = gain_ref[:, pl.ds(pl.multiple_of(own + c, 128), 128)]
                v = hv[at, pl.ds(pl.multiple_of(own + c, 128), 128)].astype(jnp.float32)
                nt[d, at, c : c + 128] = (v * sc[0, at, :] * g).astype(jnp.bfloat16)
                v = pr[at, pl.ds(pl.multiple_of(got + c, 128), 128)].astype(jnp.float32)
                nt[d, low, c : c + 128] = (v * sc[1, at, :] * g).astype(jnp.bfloat16)
            return carry

        lax.fori_loop(0, tokens // 64, norm_rows, 0)
        acc[d] = jnp.dot(
            ct[0], nt[d, :tokens, :], preferred_element_type=jnp.float32
        ) + jnp.dot(ct[1], nt[d, tokens:, :], preferred_element_type=jnp.float32)

    def process(d, s):
        ft = s // ndp
        m = ndp - 1 - s % ndp
        h = flip(dp, m)
        orow = pl.ds(pl.multiple_of(h * owned, owned), owned)
        first = q == (line - 1 if d == 0 else 0)
        last = q == (0 if d == 0 else line - 1)

        @pl.when(m == ndp - 1)
        def _():
            multiply(d, ft)

        @pl.when(first)
        def _():
            sbuf[d, s] = acc[d, orow, :].astype(jnp.bfloat16)
            z_copy(d, s).start()

        @pl.when(jnp.logical_not(first | last))
        def _():
            z_copy(d, s).wait_recv()
            sbuf[d, s] = (acc[d, orow, :] + rbuf[d, s].astype(jnp.float32)).astype(jnp.bfloat16)
            z_copy(d, s).start()

        @pl.when(last)
        def _():
            z_copy(d, s).wait_recv()
            tile = acc[d, orow, :] + rbuf[d, s].astype(jnp.float32)
            fin[orow, pl.ds(pl.multiple_of(ft * fc, fc), fc)] = tile
            sqacc[...] += jnp.sum((tile * tile).reshape(owned // 8, 8, fc), axis=0)

            @pl.when(m > 0)
            def _():
                dp_copy(m, ft).start()

    def step(t, carry):
        for d in range(2):
            s = t - ((line - 1 - q) if d == 0 else q) * LAG

            @pl.when((s >= 0) & (s < chunks))
            def _():
                process(d, s)

        return carry

    lax.fori_loop(0, chunks + (line - 1) * LAG, step, 0)

    def z_done(s, carry):
        @pl.when(q > 0)
        def _():
            z_copy(0, s).wait_send()

        @pl.when(q < line - 1)
        def _():
            z_copy(1, s).wait_send()

        return carry

    rc = 256
    rtiles = block // rc

    def rel_copy(i, to):
        at = pl.ds(i * rc, rc)
        return pltpu.make_async_remote_copy(
            src_ref=relsend.at[at], dst_ref=relrecv.at[at], send_sem=rs.at[i], recv_sem=rr.at[i],
            device_id=(dp, to), device_id_type=MESH,
        )

    def ending(sd):
        toward = up if sd == 0 else down
        weight = w_ref[0, 0] * inv_len
        sq = jnp.sum(jnp.sum(sqacc[...], axis=1, keepdims=True), axis=0, keepdims=True)
        row = lax.broadcasted_iota(jnp.int32, (8, 128), 0)
        sqbuf[0] = jnp.where(row == 0, jnp.broadcast_to(sq * (weight * weight), (8, 128)), weight)
        sends = [
            pltpu.make_async_remote_copy(
                src_ref=sqbuf.at[0], dst_ref=sqbuf.at[slot], send_sem=ss.at[slot - 1],
                recv_sem=sr.at[slot - 1], device_id=peer, device_id_type=MESH,
            )
            for slot, peer in ends
        ]
        for c in sends:
            c.start()
        lax.fori_loop(0, chunks, z_done, 0)
        for m in range(1, ndp):
            lax.fori_loop(0, ftiles, lambda ft, c, m=m: (dp_copy(m, ft).wait(), c)[1], 0)
        for c in sends:
            c.wait()
        mult = []
        for a in range(ndp):
            base = a * 2 * CORES
            total = sqbuf[base, 0:1, :]
            for i in range(1, 2 * CORES):
                total = total + sqbuf[base + i, 0:1, :]
            factor = jnp.minimum(1.0, bound * lax.rsqrt(total + 1e-06))
            mult.append((factor * sqbuf[base, 1:2, :])[:, 0:1])
        mine = pl.ds(pl.multiple_of(dp * owned, owned), owned)

        def combine(f0):
            cols = slice(f0, f0 + rc)
            value = fin[mine, cols] * mult[0]
            for m in range(1, ndp):
                value = value + dpbuf[m - 1, :, cols] * mult[m]
            return value.T

        far, near = (block, 0) if sd == 0 else (0, block)
        for i in range(rtiles):
            relsend[i * rc : (i + 1) * rc, :] = combine(far + i * rc).astype(relsend.dtype)
            rel_copy(i, toward).start()
        for i in range(rtiles):
            out_ref[i * rc : (i + 1) * rc, :] = combine(near + i * rc)
        for i in range(rtiles):
            rel_copy(i, toward).wait_send()

    @pl.when(q == 0)
    def _():
        ending(0)

    @pl.when(q == line - 1)
    def _():
        ending(1)

    @pl.when(jnp.logical_not(is_end))
    def _():
        lax.fori_loop(0, chunks, z_done, 0)
        for i in range(rtiles):
            rel_copy(i, down).wait_recv()
            out_ref[i * rc : (i + 1) * rc, :] = relrecv[i * rc : (i + 1) * rc, :].astype(jnp.float32)


def fused(hidden, norm_gain, cotangent, loss_weight):
    _, tokens, features = hidden.shape
    outs = cotangent.shape[2]
    ctx = lax.axis_size("ctx")
    ndp = lax.axis_size("dp")
    line = ctx // CORES
    block = features // ctx
    half = features // CORES // 2
    owned = outs // ndp
    fc, rows, groups, pieces = 256, 16, 8, 4
    ftiles = half // fc
    chunks = ftiles * ndp
    cfg = (tokens, features, outs, line, ndp, fc, rows,
           1.0 / math.sqrt(tokens * ctx), math.sqrt(features * outs))
    bf16, f32 = jnp.bfloat16, jnp.float32
    dma = pltpu.SemaphoreType.DMA
    vmem = pl.BlockSpec(memory_space=pltpu.VMEM)
    return pl.pallas_call(
        functools.partial(kernel, cfg),
        name="clipped_grad",
        out_shape=jax.ShapeDtypeStruct((block, owned), f32),
        in_specs=[pl.BlockSpec(memory_space=pl.ANY), vmem, vmem,
                  pl.BlockSpec(memory_space=pltpu.SMEM)],
        out_specs=vmem,
        scratch_shapes=[
            pltpu.VMEM((tokens, features), bf16),
            pltpu.VMEM((tokens, features // CORES), bf16),
            pltpu.VMEM((CORES, outs, tokens), bf16),
            pltpu.VMEM((CORES, tokens, 128), f32),
            pltpu.VMEM((2, CORES * tokens, fc), bf16),
            pltpu.VMEM((2, outs, fc), f32),
            pltpu.VMEM((2, chunks, owned, fc), bf16),
            pltpu.VMEM((2, chunks, owned, fc), bf16),
            pltpu.VMEM((outs, half), f32),
            pltpu.VMEM((ndp - 1, owned, half), f32),
            pltpu.VMEM((8, fc), f32),
            pltpu.VMEM((ndp * 2 * CORES, 8, 128), f32),
            pltpu.VMEM((block, owned), bf16),
            pltpu.VMEM((block, owned), bf16),
            dma((groups,)),
            dma((2 * pieces,)), dma((2 * pieces,)),
            dma((2,)), dma((2,)),
            dma((2, chunks)), dma((2, chunks)),
            dma((ndp - 1, ftiles)), dma((ndp - 1, ftiles)),
            dma((ndp * 2 * CORES - 1,)), dma((ndp * 2 * CORES - 1,)),
            dma((block // 256,)), dma((block // 256,)),
        ],
        compiler_params=pltpu.CompilerParams(
            collective_id=0, has_side_effects=True, vmem_limit_bytes=60 << 20
        ),
    )(hidden[0], norm_gain[None, :], cotangent[0], loss_weight[None, :])


def solution(mesh):
    in_specs = (P("dp", "ctx", None), P(), P("dp", "ctx", None), P("dp"))
    out_specs = P("ctx", "dp")
    short = mesh.shape["ctx"] == 4 * CORES and mesh.shape["dp"] == 4
    body = fused if short else per_device
    return jax.shard_map(body, mesh=mesh, in_specs=in_specs, out_specs=out_specs, check_vma=False)
```

```python
import functools
import math

import jax
import jax.numpy as jnp
from jax import lax
from jax.experimental import pallas as pl
from jax.experimental.pallas import tpu as pltpu
from jax.sharding import PartitionSpec as P

MESH = pl.DeviceIdType.MESH
CORES = 2
LAG = 3
SPLIT = 1
AHEAD = 2


def per_device(hidden, norm_gain, cotangent, loss_weight):
    widened = hidden[0].astype(jnp.float32)
    scale = lax.rsqrt(jnp.mean(widened * widened, axis=1, keepdims=True) + 1e-05)
    normed = (widened * scale * norm_gain).astype(jnp.bfloat16)
    upstream = cotangent[0]
    context_size = lax.axis_size("ctx")
    doc_length = upstream.shape[0] * context_size
    weight = loss_weight[0] / math.sqrt(doc_length)
    features = normed.shape[1]
    outputs = upstream.shape[1]
    contract = (((0,), (0,)), ((), ()))
    owned_tile = lax.psum_scatter(
        weight * lax.dot_general(normed, upstream, contract, preferred_element_type=jnp.float32),
        "ctx",
        scatter_dimension=0,
        tiled=True,
    )
    squares = jnp.sum(owned_tile * owned_tile)
    clip_bound = math.sqrt(features * outputs)
    summed = lax.psum(squares, "ctx")
    factor = jnp.minimum(1.0, clip_bound * lax.rsqrt(summed + 1e-06))
    result = lax.psum_scatter(factor * owned_tile, "dp", scatter_dimension=1, tiled=True)
    return result


def flip(v, m):
    return ((v // 2 + m // 2) % 2) * 2 + (v % 2 + m % 2) % 2


def kernel(
    cfg,
    hid_ref,
    gain_ref,
    cot_ref,
    w_ref,
    out_ref,
    hv,
    pr,
    ct,
    sc,
    nt,
    acc,
    sbuf,
    rbuf,
    fin,
    dpbuf,
    sqacc,
    sqbuf,
    wide_s,
    wide_r,
    slim_s,
    slim_r,
    ls,
    xs,
    xr,
    es,
    er,
    zs,
    zr,
    ds_,
    dr,
    ss,
    sr,
    rs,
    rr,
):
    (tokens, features, outs, line, ndp, fc, rows, inv_len, bound) = cfg
    block = features // (CORES * line)
    half = features // CORES // 2
    ftiles = half // fc
    owned = outs // ndp
    chunks = ftiles * ndp * SPLIT
    part = owned // SPLIT
    groups = ls.shape[0]
    grows = tokens // groups
    dp = lax.axis_index("dp")
    ctx = lax.axis_index("ctx")
    q = ctx // CORES
    k = ctx % CORES
    other = ctx - k + (1 - k)
    side = q // (line - 1)
    is_end = (q == 0) | (q == line - 1)
    down = ctx - CORES
    up = ctx + CORES

    ends = []
    for a in range(ndp):
        for b in range(2):
            for c in range(CORES):
                if a + b + c > 0:
                    pos = ((side + b) % 2) * (line - 1) * CORES + (k + c) % CORES
                    ends.append(((a * 2 + b) * CORES + c, (flip(dp, a), pos)))

    bar = pltpu.get_barrier_semaphore()
    pl.semaphore_signal(bar, inc=1, device_id=(dp, other), device_id_type=MESH)

    @pl.when(q > 0)
    def _():
        pl.semaphore_signal(bar, inc=1, device_id=(dp, down), device_id_type=MESH)

    @pl.when(q < line - 1)
    def _():
        pl.semaphore_signal(bar, inc=1, device_id=(dp, up), device_id_type=MESH)

    @pl.when(is_end)
    def _():
        for slot, peer in ends:
            if slot != 1:
                pl.semaphore_signal(bar, inc=1, device_id=peer, device_id_type=MESH)

    def load(g):
        at = pl.ds(pl.multiple_of(g * grows, grows), grows)
        return pltpu.make_async_copy(hid_ref.at[at], hv.at[at], ls.at[g])

    for g in range(groups):
        load(g).start()
    ct[0] = cot_ref[...].T

    @pl.when(is_end)
    def _():
        pl.semaphore_wait(bar, len(ends) + 1)

    @pl.when(jnp.logical_not(is_end))
    def _():
        pl.semaphore_wait(bar, 3)

    def place(d, local, core):
        return (CORES * (d * (line // 2) + local // block) + core) * block + local % block

    def piece_copy(d, p):
        src = pl.ds(pl.multiple_of(place(d, p * fc, 1 - k), fc), fc)
        dst = pl.ds(pl.multiple_of(d * half + p * fc, fc), fc)
        return pltpu.make_async_remote_copy(
            src_ref=hid_ref.at[:, src], dst_ref=pr.at[:, dst],
            send_sem=xs.at[2 * p + d], recv_sem=xr.at[2 * p + d],
            device_id=(dp, other), device_id_type=MESH,
        )

    def extra_copy(buf, i):
        return pltpu.make_async_remote_copy(
            src_ref=buf.at[0], dst_ref=buf.at[1], send_sem=es.at[i], recv_sem=er.at[i],
            device_id=(dp, other), device_id_type=MESH,
        )

    for p in range(AHEAD):
        for d in range(2):
            piece_copy(d, p).start()
        if p == 0:
            extra_copy(ct, 0).start()

    def stat_rows(i, carry):
        at = pl.ds(pl.multiple_of(i * rows, rows), rows)
        total = jnp.zeros((rows, block), jnp.float32)
        for j in range(CORES * line):
            v = hv[at, j * block : (j + 1) * block].astype(jnp.float32)
            total = total + v * v
        mean = jnp.sum(total, axis=1, keepdims=True) * (1.0 / features)
        sc[0, at, :] = jnp.broadcast_to(lax.rsqrt(mean + 1e-05), (rows, 128))
        return carry

    def stat_group(g, carry):
        load(g).wait()
        per = grows // rows
        lax.fori_loop(g * per, (g + 1) * per, stat_rows, 0)
        return carry

    lax.fori_loop(0, groups, stat_group, 0)
    extra_copy(sc, 1).start()
    sqacc[...] = jnp.zeros_like(sqacc)
    extra_copy(ct, 0).wait()
    extra_copy(sc, 1).wait()

    def z_copy(d, s):
        return pltpu.make_async_remote_copy(
            src_ref=sbuf.at[d, s], dst_ref=rbuf.at[d, s], send_sem=zs.at[d, s],
            recv_sem=zr.at[d, s], device_id=(dp, down if d == 0 else up), device_id_type=MESH,
        )

    def dp_copy(m, ft):
        h = flip(dp, m)
        cols = pl.ds(pl.multiple_of(ft * fc, fc), fc)
        return pltpu.make_async_remote_copy(
            src_ref=fin.at[pl.ds(pl.multiple_of(h * owned, owned), owned), cols],
            dst_ref=dpbuf.at[m - 1, :, cols],
            send_sem=ds_.at[m - 1, ft], recv_sem=dr.at[m - 1, ft],
            device_id=(h, ctx), device_id_type=MESH,
        )

    def multiply(d, ft):
        @pl.when(ft + AHEAD < ftiles)
        def _():
            piece_copy(d, ft + AHEAD).start()

        piece_copy(d, ft).wait()
        own = pl.multiple_of(place(d, ft * fc, k), fc)
        got = pl.multiple_of(d * half + ft * fc, fc)

        def norm_rows(i, carry):
            at = pl.ds(pl.multiple_of(i * 64, 64), 64)
            low = pl.ds(pl.multiple_of(tokens + i * 64, 64), 64)
            for c in range(0, fc, 128):
                g = gain_ref[:, pl.ds(pl.multiple_of(own + c, 128), 128)]
                v = hv[at, pl.ds(pl.multiple_of(own + c, 128), 128)].astype(jnp.float32)
                nt[d, at, c : c + 128] = (v * sc[0, at, :] * g).astype(jnp.bfloat16)
                v = pr[at, pl.ds(pl.multiple_of(got + c, 128), 128)].astype(jnp.float32)
                nt[d, low, c : c + 128] = (v * sc[1, at, :] * g).astype(jnp.bfloat16)
            return carry

        lax.fori_loop(0, tokens // 64, norm_rows, 0)
        acc[d] = jnp.dot(
            ct[0], nt[d, :tokens, :], preferred_element_type=jnp.float32
        ) + jnp.dot(ct[1], nt[d, tokens:, :], preferred_element_type=jnp.float32)

    def process(d, s):
        ft = s // (ndp * SPLIT)
        m = ndp - 1 - s // SPLIT % ndp
        u = s % SPLIT
        h = flip(dp, m)
        orow = pl.ds(pl.multiple_of(h * owned + u * part, part), part)
        first = q == (line - 1 if d == 0 else 0)
        last = q == (0 if d == 0 else line - 1)

        @pl.when((m == ndp - 1) & (u == 0))
        def _():
            multiply(d, ft)

        @pl.when(first)
        def _():
            sbuf[d, s] = acc[d, orow, :].astype(jnp.bfloat16)
            z_copy(d, s).start()

        @pl.when(jnp.logical_not(first | last))
        def _():
            z_copy(d, s).wait_recv()
            sbuf[d, s] = (acc[d, orow, :] + rbuf[d, s].astype(jnp.float32)).astype(jnp.bfloat16)
            z_copy(d, s).start()

        @pl.when(last)
        def _():
            z_copy(d, s).wait_recv()
            tile = acc[d, orow, :] + rbuf[d, s].astype(jnp.float32)
            fin[orow, pl.ds(pl.multiple_of(ft * fc, fc), fc)] = tile
            sqacc[...] += jnp.sum((tile * tile).reshape(part // 8, 8, fc), axis=0)

            @pl.when((m > 0) & (u == SPLIT - 1))
            def _():
                dp_copy(m, ft).start()

    def step(t, carry):
        for d in range(2):
            s = t - ((line - 1 - q) if d == 0 else q) * LAG

            @pl.when((s >= 0) & (s < chunks))
            def _():
                process(d, s)

        return carry

    lax.fori_loop(0, chunks + (line - 1) * LAG, step, 0)

    def z_done(s, carry):
        @pl.when(q > 0)
        def _():
            z_copy(0, s).wait_send()

        @pl.when(q < line - 1)
        def _():
            z_copy(1, s).wait_send()

        return carry

    rc = 256
    rtiles = block // rc

    def relay(i):
        if i < rtiles // 2:
            return wide_s, wide_r, pl.ds(i * rc, rc)
        return slim_s, slim_r, pl.ds((i - rtiles // 2) * rc, rc)

    def rel_copy(i, to):
        src, dst, at = relay(i)
        return pltpu.make_async_remote_copy(
            src_ref=src.at[at], dst_ref=dst.at[at], send_sem=rs.at[i], recv_sem=rr.at[i],
            device_id=(dp, to), device_id_type=MESH,
        )

    def ending(sd):
        toward = up if sd == 0 else down
        weight = w_ref[0, 0] * inv_len
        sq = jnp.sum(jnp.sum(sqacc[...], axis=1, keepdims=True), axis=0, keepdims=True)
        row = lax.broadcasted_iota(jnp.int32, (8, 128), 0)
        sqbuf[0] = jnp.where(row == 0, jnp.broadcast_to(sq * (weight * weight), (8, 128)), weight)
        sends = [
            pltpu.make_async_remote_copy(
                src_ref=sqbuf.at[0], dst_ref=sqbuf.at[slot], send_sem=ss.at[slot - 1],
                recv_sem=sr.at[slot - 1], device_id=peer, device_id_type=MESH,
            )
            for slot, peer in ends
        ]
        for c in sends:
            c.start()
        lax.fori_loop(0, chunks, z_done, 0)
        for m in range(1, ndp):
            lax.fori_loop(0, ftiles, lambda ft, c, m=m: (dp_copy(m, ft).wait(), c)[1], 0)
        for c in sends:
            c.wait()
        mult = []
        for a in range(ndp):
            base = a * 2 * CORES
            total = sqbuf[base, 0:1, :]
            for i in range(1, 2 * CORES):
                total = total + sqbuf[base + i, 0:1, :]
            factor = jnp.minimum(1.0, bound * lax.rsqrt(total + 1e-06))
            mult.append((factor * sqbuf[base, 1:2, :])[:, 0:1])
        mine = pl.ds(pl.multiple_of(dp * owned, owned), owned)

        def combine(f0):
            cols = slice(f0, f0 + rc)
            value = fin[mine, cols] * mult[0]
            for m in range(1, ndp):
                value = value + dpbuf[m - 1, :, cols] * mult[m]
            return value.T

        far, near = (block, 0) if sd == 0 else (0, block)
        for i in range(rtiles):
            src, _, at = relay(i)
            src[at, :] = combine(far + i * rc).astype(src.dtype)
            rel_copy(i, toward).start()
        for i in range(rtiles):
            out_ref[i * rc : (i + 1) * rc, :] = combine(near + i * rc)
        for i in range(rtiles):
            rel_copy(i, toward).wait_send()

    @pl.when(q == 0)
    def _():
        ending(0)

    @pl.when(q == line - 1)
    def _():
        ending(1)

    @pl.when(jnp.logical_not(is_end))
    def _():
        lax.fori_loop(0, chunks, z_done, 0)
        for i in range(rtiles):
            rel_copy(i, down).wait_recv()
            _, got, at = relay(i)
            out_ref[i * rc : (i + 1) * rc, :] = got[at, :].astype(jnp.float32)


def fused(hidden, norm_gain, cotangent, loss_weight):
    _, tokens, features = hidden.shape
    outs = cotangent.shape[2]
    ctx = lax.axis_size("ctx")
    ndp = lax.axis_size("dp")
    line = ctx // CORES
    block = features // ctx
    half = features // CORES // 2
    owned = outs // ndp
    fc, rows, groups = 256, 16, 8
    ftiles = half // fc
    chunks = ftiles * ndp * SPLIT
    cfg = (tokens, features, outs, line, ndp, fc, rows,
           1.0 / math.sqrt(tokens * ctx), math.sqrt(features * outs))
    bf16, f32 = jnp.bfloat16, jnp.float32
    dma = pltpu.SemaphoreType.DMA
    vmem = pl.BlockSpec(memory_space=pltpu.VMEM)
    return pl.pallas_call(
        functools.partial(kernel, cfg),
        name="clipped_grad",
        out_shape=jax.ShapeDtypeStruct((block, owned), f32),
        in_specs=[pl.BlockSpec(memory_space=pl.ANY), vmem, vmem,
                  pl.BlockSpec(memory_space=pltpu.SMEM)],
        out_specs=vmem,
        scratch_shapes=[
            pltpu.VMEM((tokens, features), bf16),
            pltpu.VMEM((tokens, features // CORES), bf16),
            pltpu.VMEM((CORES, outs, tokens), bf16),
            pltpu.VMEM((CORES, tokens, 128), f32),
            pltpu.VMEM((2, CORES * tokens, fc), bf16),
            pltpu.VMEM((2, outs, fc), f32),
            pltpu.VMEM((2, chunks, owned // SPLIT, fc), bf16),
            pltpu.VMEM((2, chunks, owned // SPLIT, fc), bf16),
            pltpu.VMEM((outs, half), f32),
            pltpu.VMEM((ndp - 1, owned, half), f32),
            pltpu.VMEM((8, fc), f32),
            pltpu.VMEM((ndp * 2 * CORES, 8, 128), f32),
            pltpu.VMEM((block // 2, owned), f32),
            pltpu.VMEM((block // 2, owned), f32),
            pltpu.VMEM((block // 2, owned), bf16),
            pltpu.VMEM((block // 2, owned), bf16),
            dma((groups,)),
            dma((2 * ftiles,)), dma((2 * ftiles,)),
            dma((2,)), dma((2,)),
            dma((2, chunks)), dma((2, chunks)),
            dma((ndp - 1, ftiles)), dma((ndp - 1, ftiles)),
            dma((ndp * 2 * CORES - 1,)), dma((ndp * 2 * CORES - 1,)),
            dma((block // 256,)), dma((block // 256,)),
        ],
        compiler_params=pltpu.CompilerParams(
            collective_id=0, has_side_effects=True, vmem_limit_bytes=60 << 20
        ),
    )(hidden[0], norm_gain[None, :], cotangent[0], loss_weight[None, :])


def solution(mesh):
    in_specs = (P("dp", "ctx", None), P(), P("dp", "ctx", None), P("dp"))
    out_specs = P("ctx", "dp")
    short = mesh.shape["ctx"] == 4 * CORES and mesh.shape["dp"] == 4
    body = fused if short else per_device
    return jax.shard_map(body, mesh=mesh, in_specs=in_specs, out_specs=out_specs, check_vma=False)
```
